32 devices in a mesh: section: 4 (over z), dp: 8 (over y, x, core).
Axes of the slice: x: 2, y: 2, z: 4, core: 2. Of those that a mesh axis runs over, the one named last changes fastest.
Arguments:
- gradient: float32 [4, 8, 256, 4096], P('section', 'dp'), may hold values from -6 to 6
- dither: int32 [4, 8, 256, 4096], P('section', 'dp'), may hold values from 0 to 255
- sign_bits: int32 [4096], replicated, may hold values from 0 to 1
- levels: float32 [16], replicated, may hold values from -1 to 1, as said below
- layout: int32 [256], replicated, may hold values from 0 to 255, each once
- master: float32 [4, 256, 4096], P('section', 'dp'), may hold values from -6 to 6
- first_moment: float32 [4, 256, 4096], P('section', 'dp'), may hold values from -4 to 4
- second_moment: float32 [4, 256, 4096], P('section', 'dp'), may hold values from 0.05 to 2
Outputs:
- updated_master: float32 [4, 256, 4096], P('section', 'dp')
- updated_first: float32 [4, 256, 4096], P('section', 'dp')
- updated_second: float32 [4, 256, 4096], P('section', 'dp')
- parameters: bfloat16 [4, 256, 4096], P('section')
The draws below stay inside these ranges and needn't reach their ends.
Inputs may be any that keep to these rules, and one draw needn't show every extreme that they name: `levels`: strictly increasing; the first is -1 and the last 1; neighbouring levels differ by at least 1/30. `layout`: each block number once.
All inputs are finite; a program needn't handle non-finite values.
Results may differ from the reference program's by a relative error of at most 0.001.
The reference program's roundings to bfloat16 on the way (of `symbols`) count: a program that leaves them out, or rounds other values in their place, can miss the bound.
Values may be sent and summed in bfloat16 or wider, within the bound.
A program may use at most 64 MiB of HBM per device.

```python
import math
import jax
import jax.numpy as jnp
from jax import lax

LEVELS = 16
BLOCK = 4096
BLOCKS = 256
N_SECTION = 4
N_DP = 8


def draw_levels(key, part):
    spacing = jax.random.uniform(key, (LEVELS - 1,), jnp.float32, 1.0, 4.0)
    rising = jnp.concatenate([jnp.zeros((1,), jnp.float32), jnp.cumsum(spacing)])
    return -1.0 + 2.0 * rising / rising[-1]


def plant(values, stream_key, least, high):
    dims = values.shape
    spot = [jax.random.randint(jax.random.fold_in(stream_key, axis), (), 0, dims[axis]) for axis in range(len(dims))]
    values = values.at[tuple(spot)].set(least)
    longest = dims.index(max(dims))
    spot[longest] = (spot[longest] + 1) % dims[longest]
    return values.at[tuple(spot)].set(high)


def steps_of(key, extent, pieces, low, top_value):
    gain, own = 1.0, jax.random.fold_in(key, 6)
    for axis_at, shards_of in pieces:
        heights = jnp.exp(jax.random.uniform(jax.random.fold_in(own, axis_at), (shards_of,), jnp.float32, low / len(pieces), top_value / len(pieces)))
        gain = gain * jnp.repeat(heights, extent[axis_at] // shards_of).reshape([-1 if axis == axis_at else 1 for axis in range(len(extent))])
    return gain


def bell_draw(stream_key, dims, width, most, shards=(), held_as=jnp.bfloat16):
    array = width * jax.random.normal(stream_key, dims, jnp.float32)
    if shards:
        array = array * steps_of(stream_key, dims, shards, -0.22, 0.18)
    return jnp.clip(array, -most, most).astype(held_as)


def setup_inputs(seed: int = 0) -> dict:
    splits = jax.random.split(jax.random.key(seed), 9)
    return {
        "gradient": bell_draw(splits[0], (N_SECTION, N_DP, BLOCKS, BLOCK), 1.0, 6.0, ((0, 4), (1, 8)), jnp.float32),
        "dither": plant(jax.random.randint(splits[1], (N_SECTION, N_DP, BLOCKS, BLOCK), 0, 256), jax.random.fold_in(splits[1], 1), 0, 255).astype(jnp.int32),
        "sign_bits": plant(jax.random.randint(splits[2], (BLOCK,), 0, 2), jax.random.fold_in(splits[2], 1), 0, 1).astype(jnp.int32),
        "levels": draw_levels(jax.random.fold_in(splits[8], 71), 0),
        "layout": jax.random.permutation(splits[4], BLOCKS).astype(jnp.int32),
        "master": bell_draw(splits[5], (N_SECTION, BLOCKS, BLOCK), 1.0, 6.0, ((0, 4), (1, 8)), jnp.float32),
        "first_moment": bell_draw(splits[6], (N_SECTION, BLOCKS, BLOCK), 0.5, 4.0, ((0, 4), (1, 8)), jnp.float32),
        "second_moment": jnp.clip(jnp.exp(math.log(2.0) - 3.6888794 * jax.random.uniform(splits[7], (N_SECTION, BLOCKS, BLOCK), jnp.float32) ** steps_of(splits[7], (N_SECTION, BLOCKS, BLOCK), ((0, 4), (1, 8)), -0.2, 0.2)), 0.05, 2.0),
    }


adam_epsilon = 1e-08
learning_rate = 0.02
weight_decay = 0.1
first_decay = 0.9
second_decay = 0.95
dither_steps = 256.0

def hadamard_table(edge_length):
    row_numbers = lax.broadcasted_iota(jnp.int32, (edge_length, edge_length), 0)
    column_numbers = lax.broadcasted_iota(jnp.int32, (edge_length, edge_length), 1)
    common = jnp.bitwise_and(row_numbers, column_numbers)
    parity = jnp.zeros((edge_length, edge_length), jnp.int32)
    for bit_number in range(edge_length.bit_length() - 1):
        parity = parity + jnp.bitwise_and(jnp.right_shift(common, bit_number), 1)
    parity = parity % 2
    return (1 - 2 * parity).astype(jnp.float32)

def square_transform(blocks):
    edge_length = math.isqrt(blocks.shape[-1])
    table = hadamard_table(edge_length)
    folded = blocks.reshape(-1, edge_length, edge_length)
    turned = jnp.einsum('ac,ncd,db->nab', table, folded, table, precision=lax.Precision.HIGHEST)
    return turned.reshape(blocks.shape) / edge_length

def rotate(blocks, flips):
    return square_transform(blocks * flips)

def unrotate(blocks, flips):
    return square_transform(blocks) * flips

def encode(ratios, levels):
    relaxed = jnp.zeros_like(ratios)
    for position in range(levels.shape[0] - 1):
        spacing = levels[position + 1] - levels[position]
        relaxed = relaxed + jnp.clip((ratios - levels[position]) / spacing, 0.0, 1.0)
    return relaxed

def decode(symbols, levels):
    values = jnp.zeros_like(symbols) + levels[0]
    for position in range(levels.shape[0] - 1):
        spacing = levels[position + 1] - levels[position]
        values = values + spacing * jnp.clip(symbols - position, 0.0, 1.0)
    return values

def reference(gradient, dither, sign_bits, levels, layout, master, first_moment, second_moment):
    flips = (1 - 2 * sign_bits).astype(jnp.float32)
    stacked = gradient.reshape(N_SECTION * N_DP, BLOCKS, BLOCK)
    peaks = lax.map(lambda single: lax.optimization_barrier(jnp.max(jnp.abs(rotate(single, flips)), axis=1)), stacked)
    block_scale = lax.optimization_barrier(jnp.max(peaks.reshape(N_SECTION, N_DP, BLOCKS), axis=1)) + 1e-06
    inverse = jnp.argsort(layout).astype(jnp.int32)
    section_grads = []
    for section_number in range(N_SECTION):
        scale_here = block_scale[section_number]

        def accumulate(carry, inputs):
            single, noise = inputs
            ratios = rotate(single, flips) / scale_here[:, None]
            offsets = (noise.astype(jnp.float32) + 0.5) / dither_steps - 0.5
            symbols = (encode(ratios, levels) + offsets).astype(jnp.bfloat16)
            return (carry + decode(symbols.astype(jnp.float32), levels), None)
        summed_codes, _ = lax.scan(accumulate, jnp.zeros((BLOCKS, BLOCK), jnp.float32), (gradient[section_number], dither[section_number]))
        slot_sums = jnp.take(summed_codes, layout, axis=0) * jnp.take(scale_here, layout)[:, None]
        section_grads.append(unrotate(slot_sums, flips))
    grads = jnp.stack(section_grads)
    updated_first = first_decay * first_moment + (1.0 - first_decay) * grads
    updated_second = second_decay * second_moment + (1.0 - second_decay) * grads * grads
    updated_master = master - learning_rate * (updated_first / (jnp.sqrt(updated_second) + adam_epsilon) + weight_decay * master)
    parameters = jnp.take(updated_master.astype(jnp.bfloat16), inverse, axis=1)
    return (updated_master, updated_first, updated_second, parameters)
```

```python
import functools
import math

import jax
import jax.numpy as jnp
from jax import lax
from jax.experimental import pallas as pl
from jax.experimental.pallas import tpu as pltpu
from jax.sharding import PartitionSpec as P

MESH = pl.DeviceIdType.MESH
adam_epsilon = 1e-08
learning_rate = 0.02
weight_decay = 0.1
first_decay = 0.9
second_decay = 0.95
dither_steps = 256.0
CHUNKS = 4
LANES = 128
TILE = 256
VMEM_LIMIT = 60 * 1024 * 1024


def hadamard(edge, scale):
    rows = lax.broadcasted_iota(jnp.int32, (edge, edge), 0)
    columns = lax.broadcasted_iota(jnp.int32, (edge, edge), 1)
    common = rows & columns
    parity = jnp.zeros((edge, edge), jnp.int32)
    for bit in range(edge.bit_length() - 1):
        parity = parity + ((common >> bit) & 1)
    return ((1 - 2 * (parity & 1)).astype(jnp.float32) * scale).astype(jnp.bfloat16)


def exact_dot(x, table):
    high = x.astype(jnp.bfloat16)
    rest = x - high.astype(jnp.float32)
    middle = rest.astype(jnp.bfloat16)
    low = (rest - middle.astype(jnp.float32)).astype(jnp.bfloat16)
    dot = functools.partial(jnp.dot, preferred_element_type=jnp.float32)
    return dot(high, table) + (dot(middle, table) + dot(low, table))


def butterflies(pieces):
    pieces = list(pieces)
    step = 1
    while step < len(pieces):
        for i in range(len(pieces)):
            if not i & step:
                a, b = pieces[i], pieces[i + step]
                pieces[i], pieces[i + step] = a + b, a - b
        step *= 2
    return pieces


def transform(pieces, table):
    rows = pieces[0].shape[0]
    turned = exact_dot(jnp.concatenate(pieces, axis=0), table)
    return butterflies([turned[c * rows : (c + 1) * rows] for c in range(len(pieces))])


def lookup(table, index):
    return jnp.take_along_axis(
        jnp.broadcast_to(table, index.shape), index, axis=1, mode="promise_in_bounds"
    )


def level_rows(levels_ref, count):
    lane = lax.broadcasted_iota(jnp.int32, (1, LANES), 1)
    here = jnp.zeros((1, LANES), jnp.float32)
    after = jnp.zeros((1, LANES), jnp.float32)
    for k in range(count):
        here = jnp.where(lane == k, levels_ref[k], here)
        after = jnp.where(lane == k, levels_ref[min(k + 1, count - 1)], after)
    return lane, here, after


def step_kernel(
    n, grad_hbm, dith_hbm, sign_ref, levels_ref, layout_ref, mst_hbm, fm_hbm, sm_hbm,
    um_hbm, uf_hbm, us_hbm, gall,
    x, dith, rot, pmat, hmat, flip, peaks, pk_send, pk_recv, symt, sym, symr, sums,
    mst, fm, sm, um, uf, us, pr,
    load_sem, dith_sem, side_sem, pks_sem, pkr_sem, as_sem, ar_sem, gs_sem, gr_sem, rs_sem, rr_sem,
):
    me = lax.axis_index("dp")
    blocks, size = x.shape
    own = blocks // n
    tiles = size // TILE
    per = tiles // CHUNKS
    rows = blocks // load_sem.shape[0]
    chips = n // 2
    chip, core = me // 2, lax.rem(me, 2)
    partner = chip * 2 + 1 - core
    count = levels_ref.shape[0]

    def load(i):
        part = pl.ds(pl.multiple_of(i * rows, rows), rows)
        return pltpu.make_async_copy(grad_hbm.at[part], x.at[part], load_sem.at[i])

    for i in range(blocks // rows):
        load(i).start()

    def load_dither(t):
        return pltpu.make_async_copy(
            dith_hbm.at[:, t * TILE : (t + 1) * TILE], dith.at[t], dith_sem.at[t]
        )

    for t in range(tiles):
        load_dither(t).start()
    sides = [
        pltpu.make_async_copy(src, dst, side_sem.at[i])
        for i, (src, dst) in enumerate(((mst_hbm, mst), (fm_hbm, fm), (sm_hbm, sm)))
    ]
    for side in sides:
        side.start()

    barrier = pltpu.get_barrier_semaphore()

    def greet(k, carry):
        pl.semaphore_signal(barrier, inc=1, device_id={"dp": lax.rem(me + k, n)}, device_id_type=MESH)
        return carry

    lax.fori_loop(1, n, greet, 0)

    flip[...] = (1 - 2 * sign_ref[...]).astype(jnp.float32)
    hmat[...] = hadamard(TILE, 1.0 / math.isqrt(size))
    block_row = lax.broadcasted_iota(jnp.int32, (blocks, blocks), 0)
    block_col = lax.broadcasted_iota(jnp.int32, (blocks, blocks), 1)
    turned_p = (block_row == layout_ref[...]).astype(jnp.float32)
    pmat[...] = turned_p.T

    @pl.loop(0, blocks // rows)
    def _(i):
        load(i).wait()
        part = pl.ds(pl.multiple_of(i * rows, rows), rows)
        pieces = [x[part, c * TILE : (c + 1) * TILE] * flip[:, c * TILE : (c + 1) * TILE] for c in range(tiles)]
        pieces = transform(pieces, hmat[...])
        top = jnp.abs(pieces[0])
        for c in range(tiles):
            rot[c, part] = pieces[c]
            top = jnp.maximum(top, jnp.abs(pieces[c]))
        peaks[part] = jnp.broadcast_to(jnp.max(top, axis=1, keepdims=True), (rows, LANES))

    eye = block_row == block_col
    peak_row = jnp.max(jnp.where(eye, peaks[:, :1], 0.0), axis=0, keepdims=True)
    pk_send[...] = jnp.broadcast_to(peak_row, pk_send.shape)
    pl.semaphore_wait(barrier, n - 1)

    def peak_copy(k):
        return pltpu.make_async_remote_copy(
            src_ref=pk_send, dst_ref=pk_recv.at[k], send_sem=pks_sem.at[k], recv_sem=pkr_sem.at[k],
            device_id={"dp": lax.rem(me + k, n)}, device_id_type=MESH,
        )

    def run(first, last, do):
        def body(k, carry):
            do(k)
            return carry
        lax.fori_loop(first, last, body, 0)

    run(1, n, lambda k: peak_copy(k).start())

    lane, here, after = level_rows(levels_ref, count)
    gap = after - here
    inside = lane < count - 1
    slope = jnp.where(inside, 1.0 / jnp.where(inside, gap, 1.0), 0.0)
    base = jnp.where(inside, lane.astype(jnp.float32) - here * slope, float(count - 1))
    delta = jnp.where(inside, gap, 0.0)
    start = jnp.where(inside, here - delta * lane.astype(jnp.float32), here)
    half_cells = LANES // 2
    edge = lane.astype(jnp.float32) / half_cells - 1.0
    first_index = jnp.zeros((1, LANES), jnp.int32)
    kink = jnp.full((1, LANES), 4.0, jnp.float32)
    for k in range(count - 2, 0, -1):
        first_index = first_index + (edge >= levels_ref[k]).astype(jnp.int32)
        kink = jnp.where(edge < levels_ref[k], levels_ref[k], kink)

    run(1, n, lambda k: peak_copy(k).wait_recv())
    best = pk_send[...]
    for k in range(1, n):
        best = jnp.maximum(best, pk_recv[k])
    scale_row = best[:1] + 1e-06
    scale_col = jnp.max(jnp.where(eye, scale_row, 0.0), axis=1, keepdims=True)
    peaks[...] = jnp.broadcast_to(1.0 / scale_col, peaks.shape)
    mine = pl.ds(pl.multiple_of(me * own, own), own)
    slot_scale = jnp.max(pmat[mine] * scale_row, axis=1, keepdims=True)
    perm = pmat[...].astype(jnp.bfloat16)

    def symbol_copy(q, k):
        peer = lax.rem(me + k, n)
        part = pl.ds(q * per, per)
        return pltpu.make_async_remote_copy(
            src_ref=sym.at[part, peer], dst_ref=symr.at[part, me],
            send_sem=as_sem.at[q, k], recv_sem=ar_sem.at[q, k],
            device_id={"dp": peer}, device_id_type=MESH,
        )

    group = 32
    for t in range(tiles):
        load_dither(t).wait()

    def encode(q):
        def tile(s, carry):
            t = q * per + s
            for r in range(blocks // group):
                part = slice(r * group, (r + 1) * group)
                inverse = peaks[part]
                for h in range(TILE // LANES):
                    side = slice(h * LANES, (h + 1) * LANES)
                    ratio = rot[t, part, side] * inverse
                    cell = jnp.minimum((ratio * half_cells + half_cells).astype(jnp.int32), LANES - 1)
                    cell = jnp.maximum(cell, 0)
                    at = lookup(first_index, cell) + (ratio >= lookup(kink, cell)).astype(jnp.int32)
                    relaxed = lookup(base, at) + lookup(slope, at) * ratio
                    offset = dith[t, part, side].astype(jnp.float32) * (1.0 / dither_steps) + (0.5 / dither_steps - 0.5)
                    symt[part, side] = (relaxed + offset).astype(jnp.bfloat16)
            moved = jnp.dot(perm, symt[...], preferred_element_type=jnp.float32).astype(jnp.bfloat16)
            sym[t] = moved.reshape(n, own, TILE)
            symr[t, me] = sym[t, me]
            return carry

        lax.fori_loop(0, per, tile, 0)
        run(1, n, lambda k: symbol_copy(q, k).start())

    run(0, CHUNKS, encode)

    def decode(q):
        run(1, n, lambda k: symbol_copy(q, k).wait_recv())

        def tile(s, carry):
            t = q * per + s
            for h in range(TILE // LANES):
                side = slice(h * LANES, (h + 1) * LANES)
                total = jnp.zeros((own, LANES), jnp.float32)
                for source in range(n):
                    value = symr[t, source, :, side].astype(jnp.float32)
                    value = jnp.clip(value, 0.0, float(count - 1))
                    at = value.astype(jnp.int32)
                    total = total + (lookup(start, at) + lookup(delta, at) * value)
                sums[t, :, side] = total * slot_scale
            return carry

        lax.fori_loop(0, per, tile, 0)

    run(0, CHUNKS, decode)

    for side in sides:
        side.wait()
    grads = transform([sums[c] for c in range(tiles)], hmat[...])
    for c in range(tiles):
        cut = slice(c * TILE, (c + 1) * TILE)
        grad = grads[c] * flip[:, cut]
        master = mst[:, cut]
        first = first_decay * fm[:, cut] + (1.0 - first_decay) * grad
        second = second_decay * sm[:, cut] + (1.0 - second_decay) * grad * grad
        fresh = master - learning_rate * (first / (jnp.sqrt(second) + adam_epsilon) + weight_decay * master)
        uf[:, cut] = first
        us[:, cut] = second
        um[:, cut] = fresh
        pr[:, cut] = fresh.astype(jnp.bfloat16)

    def gather_copy(c):
        peer = lax.rem(chip + c, chips) * 2 + core
        return pltpu.make_async_remote_copy(
            src_ref=pr, dst_ref=gall.at[me], send_sem=gs_sem.at[c], recv_sem=gr_sem.at[c],
            device_id={"dp": peer}, device_id_type=MESH,
        )

    def relay_copy(c):
        source = lax.rem(chip + chips - c, chips) * 2 + core
        return pltpu.make_async_remote_copy(
            src_ref=gall.at[source], dst_ref=gall.at[source], send_sem=rs_sem.at[c], recv_sem=rr_sem.at[c],
            device_id={"dp": partner}, device_id_type=MESH,
        )

    own_relay = pltpu.make_async_remote_copy(
        src_ref=pr, dst_ref=gall.at[me], send_sem=rs_sem.at[0], recv_sem=rr_sem.at[0],
        device_id={"dp": partner}, device_id_type=MESH,
    )
    run(1, chips, lambda c: gather_copy(c).start())
    own_relay.start()
    outs = [
        pltpu.make_async_copy(src, dst, side_sem.at[3 + i])
        for i, (src, dst) in enumerate(((um, um_hbm), (uf, uf_hbm), (us, us_hbm), (pr, gall.at[me])))
    ]
    for out in outs:
        out.start()

    def relay(c):
        gather_copy(c).wait_recv()
        relay_copy(c).start()

    run(1, chips, relay)
    own_relay.wait()
    run(1, chips, lambda c: relay_copy(c).wait())
    run(1, chips, lambda c: gather_copy(c).wait_send())
    run(1, n, lambda k: peak_copy(k).wait_send())

    def drain(q):
        run(1, n, lambda k: symbol_copy(q, k).wait_send())

    run(0, CHUNKS, drain)
    for out in outs:
        out.wait()


def spread_kernel(layout_ref, gall_ref, um_in, uf_in, us_in, um_out, uf_out, us_out, out_ref):
    blocks = layout_ref.shape[1]
    rows = lax.broadcasted_iota(jnp.int32, (blocks, blocks), 0)
    table = (rows == layout_ref[...]).astype(jnp.float32).astype(jnp.bfloat16)
    out_ref[...] = jnp.dot(table, gall_ref[...], preferred_element_type=jnp.float32).astype(jnp.bfloat16)
    um_out[...] = um_in[...]
    uf_out[...] = uf_in[...]
    us_out[...] = us_in[...]


def local(n, gradient, dither, sign_bits, levels, layout, master, first_moment, second_moment):
    blocks, size = gradient.shape[2:]
    own = blocks // n
    tiles = size // TILE
    row_chunks = 8
    f32, bf16 = jnp.float32, jnp.bfloat16
    hbm = pl.BlockSpec(memory_space=pl.ANY)
    vmem = pl.BlockSpec(memory_space=pltpu.VMEM)
    dma = pltpu.SemaphoreType.DMA
    layout_row = layout.reshape(1, blocks)
    shard = jax.ShapeDtypeStruct((own, size), f32)
    um, uf, us, gall = pl.pallas_call(
        functools.partial(step_kernel, n),
        out_shape=(shard, shard, shard, jax.ShapeDtypeStruct((n, own, size), bf16)),
        in_specs=[hbm, hbm, vmem, pl.BlockSpec(memory_space=pltpu.SMEM), vmem, hbm, hbm, hbm],
        out_specs=(hbm, hbm, hbm, hbm),
        scratch_shapes=[
            pltpu.VMEM((blocks, size), f32),
            pltpu.VMEM((tiles, blocks, TILE), jnp.int32),
            pltpu.VMEM((tiles, blocks, TILE), f32),
            pltpu.VMEM((blocks, blocks), f32),
            pltpu.VMEM((TILE, TILE), bf16),
            pltpu.VMEM((1, size), f32),
            pltpu.VMEM((blocks, LANES), f32),
            pltpu.VMEM((8, blocks), f32),
            pltpu.VMEM((n, 8, blocks), f32),
            pltpu.VMEM((blocks, TILE), bf16),
            pltpu.VMEM((tiles, n, own, TILE), bf16),
            pltpu.VMEM((tiles, n, own, TILE), bf16),
            pltpu.VMEM((tiles, own, TILE), f32),
            *[pltpu.VMEM((own, size), f32)] * 6,
            pltpu.VMEM((own, size), bf16),
            dma((row_chunks,)),
            dma((tiles,)),
            dma((7,)),
            dma((n,)),
            dma((n,)),
            dma((CHUNKS, n)),
            dma((CHUNKS, n)),
            dma((n // 2,)),
            dma((n // 2,)),
            dma((n // 2,)),
            dma((n // 2,)),
        ],
        compiler_params=pltpu.CompilerParams(
            collective_id=0, has_side_effects=True, vmem_limit_bytes=VMEM_LIMIT
        ),
    )(
        gradient[0, 0], dither[0, 0], sign_bits.reshape(1, size), levels, layout_row,
        master[0], first_moment[0], second_moment[0],
    )
    width = size // 4
    wide = pl.BlockSpec((blocks, width), lambda i: (0, i))
    narrow = pl.BlockSpec((own, width), lambda i: (0, i))
    um, uf, us, parameters = pl.pallas_call(
        spread_kernel,
        grid=(4,),
        out_shape=(shard, shard, shard, jax.ShapeDtypeStruct((blocks, size), bf16)),
        in_specs=[pl.BlockSpec((1, blocks), lambda i: (0, 0)), wide, narrow, narrow, narrow],
        out_specs=(narrow, narrow, narrow, wide),
    )(layout_row, gall.reshape(blocks, size), um, uf, us)
    return um[None], uf[None], us[None], parameters[None]


def solution(mesh):
    slots = P("section", "dp", None)
    streams = P("section", "dp", None, None)
    return jax.shard_map(
        functools.partial(local, mesh.shape["dp"]),
        mesh=mesh,
        in_specs=(streams, streams, P(), P(), P(), slots, slots, slots),
        out_specs=(slots, slots, slots, P("section", None, None)),
        check_vma=False,
    )
```

```python
import functools
import math

import jax
import jax.numpy as jnp
from jax import lax
from jax.experimental import pallas as pl
from jax.experimental.pallas import tpu as pltpu
from jax.sharding import PartitionSpec as P

MESH = pl.DeviceIdType.MESH
adam_epsilon = 1e-08
learning_rate = 0.02
weight_decay = 0.1
first_decay = 0.9
second_decay = 0.95
dither_steps = 256.0
CHUNKS = 8
LANES = 128
TILE = 256
VMEM_LIMIT = 60 * 1024 * 1024


def hadamard(edge, scale):
    rows = lax.broadcasted_iota(jnp.int32, (edge, edge), 0)
    columns = lax.broadcasted_iota(jnp.int32, (edge, edge), 1)
    common = rows & columns
    parity = jnp.zeros((edge, edge), jnp.int32)
    for bit in range(edge.bit_length() - 1):
        parity = parity + ((common >> bit) & 1)
    return ((1 - 2 * (parity & 1)).astype(jnp.float32) * scale).astype(jnp.bfloat16)


def exact_dot(x, table):
    high = x.astype(jnp.bfloat16)
    rest = x - high.astype(jnp.float32)
    middle = rest.astype(jnp.bfloat16)
    low = (rest - middle.astype(jnp.float32)).astype(jnp.bfloat16)
    dot = functools.partial(jnp.dot, preferred_element_type=jnp.float32)
    return dot(high, table) + (dot(middle, table) + dot(low, table))


def butterflies(pieces):
    pieces = list(pieces)
    step = 1
    while step < len(pieces):
        for i in range(len(pieces)):
            if not i & step:
                a, b = pieces[i], pieces[i + step]
                pieces[i], pieces[i + step] = a + b, a - b
        step *= 2
    return pieces


def transform(pieces, table):
    rows = pieces[0].shape[0]
    turned = exact_dot(jnp.concatenate(pieces, axis=0), table)
    return butterflies([turned[c * rows : (c + 1) * rows] for c in range(len(pieces))])


def lookup(table, index):
    return jnp.take_along_axis(
        jnp.broadcast_to(table, index.shape), index, axis=1, mode="promise_in_bounds"
    )


def piecewise(value, spots, bases, slopes):
    base = jnp.full(value.shape, bases[0], jnp.float32)
    slope = jnp.full(value.shape, slopes[0], jnp.float32)
    for spot, next_base, next_slope in zip(spots, bases[1:], slopes[1:]):
        past = value >= spot
        base = jnp.where(past, next_base, base)
        slope = jnp.where(past, next_slope, slope)
    return base + slope * value


def slot_groups(own):
    return 2 if own % 32 == 0 else 1


def level_rows(levels_ref, count):
    lane = lax.broadcasted_iota(jnp.int32, (1, LANES), 1)
    here = jnp.zeros((1, LANES), jnp.float32)
    after = jnp.zeros((1, LANES), jnp.float32)
    for k in range(count):
        here = jnp.where(lane == k, levels_ref[k], here)
        after = jnp.where(lane == k, levels_ref[min(k + 1, count - 1)], after)
    return lane, here, after


def step_kernel(
    n, grad_hbm, dith_hbm, sign_ref, levels_ref, layout_ref, mst_hbm, fm_hbm, sm_hbm,
    um_hbm, uf_hbm, us_hbm, gall,
    x, dith, rot, pmat, hmat, flip, peaks, pk_send, pk_recv, symt, sym, symr, sums,
    mst, fm, sm, um, uf, us, pr,
    load_sem, dith_sem, side_sem, pks_sem, pkr_sem, as_sem, ar_sem, gs_sem, gr_sem, rs_sem, rr_sem,
):
    me = lax.axis_index("dp")
    blocks, size = x.shape
    own = blocks // n
    tiles = size // TILE
    per = tiles // CHUNKS
    rows = blocks // load_sem.shape[0]
    chips = n // 2
    chip, core = me // 2, lax.rem(me, 2)
    partner = chip * 2 + 1 - core
    count = levels_ref.shape[0]
    groups = slot_groups(own)
    half = own // groups

    def load(i):
        part = pl.ds(pl.multiple_of(i * rows, rows), rows)
        return pltpu.make_async_copy(grad_hbm.at[part], x.at[part], load_sem.at[i])

    for i in range(blocks // rows):
        load(i).start()

    def load_dither(t):
        return pltpu.make_async_copy(
            dith_hbm.at[:, t * TILE : (t + 1) * TILE], dith.at[t], dith_sem.at[t]
        )

    for t in range(tiles):
        load_dither(t).start()
    sides = [
        pltpu.make_async_copy(src, dst, side_sem.at[i])
        for i, (src, dst) in enumerate(((mst_hbm, mst), (fm_hbm, fm), (sm_hbm, sm)))
    ]
    for side in sides:
        side.start()

    barrier = pltpu.get_barrier_semaphore()

    def greet(k, carry):
        pl.semaphore_signal(barrier, inc=1, device_id={"dp": lax.rem(me + k, n)}, device_id_type=MESH)
        return carry

    lax.fori_loop(1, n, greet, 0)

    flip[...] = (1 - 2 * sign_ref[...]).astype(jnp.float32)
    hmat[...] = hadamard(TILE, 1.0 / math.isqrt(size))
    block_row = lax.broadcasted_iota(jnp.int32, (blocks, blocks), 0)
    block_col = lax.broadcasted_iota(jnp.int32, (blocks, blocks), 1)
    turned_p = (block_row == layout_ref[...]).astype(jnp.float32)
    pmat[...] = turned_p.T

    @pl.loop(0, blocks // rows)
    def _(i):
        load(i).wait()
        part = pl.ds(pl.multiple_of(i * rows, rows), rows)
        pieces = [x[part, c * TILE : (c + 1) * TILE] * flip[:, c * TILE : (c + 1) * TILE] for c in range(tiles)]
        pieces = transform(pieces, hmat[...])
        top = jnp.abs(pieces[0])
        for c in range(tiles):
            rot[c, part] = pieces[c]
            top = jnp.maximum(top, jnp.abs(pieces[c]))
        peaks[part] = jnp.broadcast_to(jnp.max(top, axis=1, keepdims=True), (rows, LANES))

    eye = block_row == block_col
    peak_row = jnp.max(jnp.where(eye, peaks[:, :1], 0.0), axis=0, keepdims=True)
    pk_send[...] = jnp.broadcast_to(peak_row, pk_send.shape)
    pl.semaphore_wait(barrier, n - 1)

    def peak_copy(k):
        return pltpu.make_async_remote_copy(
            src_ref=pk_send, dst_ref=pk_recv.at[k], send_sem=pks_sem.at[k], recv_sem=pkr_sem.at[k],
            device_id={"dp": lax.rem(me + k, n)}, device_id_type=MESH,
        )

    def run(first, last, do):
        def body(k, carry):
            do(k)
            return carry
        lax.fori_loop(first, last, body, 0)

    run(1, n, lambda k: peak_copy(k).start())

    lane, here, after = level_rows(levels_ref, count)
    inside = lane < count - 1
    delta = jnp.where(inside, after - here, 0.0)
    start = jnp.where(inside, here - delta * lane.astype(jnp.float32), here)
    spots = [levels_ref[k] for k in range(1, count - 1)]
    gaps = [levels_ref[k + 1] - levels_ref[k] for k in range(count - 1)]
    slopes = [1.0 / gap for gap in gaps]
    bases = [float(k) - levels_ref[k] * slopes[k] for k in range(count - 1)]
    whole = [float(k) for k in range(1, count - 1)]
    starts = [levels_ref[k] - gaps[k] * float(k) for k in range(count - 1)]

    run(1, n, lambda k: peak_copy(k).wait_recv())
    best = pk_send[...]
    for k in range(1, n):
        best = jnp.maximum(best, pk_recv[k])
    scale_row = best[:1] + 1e-06
    scale_col = jnp.max(jnp.where(eye, scale_row, 0.0), axis=1, keepdims=True)
    peaks[...] = jnp.broadcast_to(1.0 / scale_col, peaks.shape)
    mine = pl.ds(pl.multiple_of(me * own, own), own)
    slot_scale = jnp.max(pmat[mine] * scale_row, axis=1, keepdims=True)
    perm = pmat[...].astype(jnp.bfloat16)

    def symbol_copy(g, q, k):
        peer = lax.rem(me + k, n)
        part = pl.ds(q * per, per)
        slots = pl.ds(g * half, half)
        return pltpu.make_async_remote_copy(
            src_ref=sym.at[part, peer, slots], dst_ref=symr.at[part, me, slots],
            send_sem=as_sem.at[g, q, k], recv_sem=ar_sem.at[g, q, k],
            device_id={"dp": peer}, device_id_type=MESH,
        )

    group = 32
    for t in range(tiles):
        load_dither(t).wait()

    def encode(q):
        def tile(s, carry):
            t = q * per + s
            for r in range(blocks // group):
                part = slice(r * group, (r + 1) * group)
                inverse = peaks[part]
                for h in range(TILE // LANES):
                    side = slice(h * LANES, (h + 1) * LANES)
                    ratio = rot[t, part, side] * inverse
                    relaxed = piecewise(ratio, spots, bases, slopes)
                    offset = dith[t, part, side].astype(jnp.float32) * (1.0 / dither_steps) + (0.5 / dither_steps - 0.5)
                    symt[part, side] = (relaxed + offset).astype(jnp.bfloat16)
            moved = jnp.dot(perm, symt[...], preferred_element_type=jnp.float32).astype(jnp.bfloat16)
            sym[t] = moved.reshape(n, own, TILE)
            symr[t, me] = sym[t, me]
            return carry

        lax.fori_loop(0, per, tile, 0)
        run(1, n, lambda k: symbol_copy(0, q, k).start())

    run(0, CHUNKS, encode)
    for g in range(1, groups):
        run(0, CHUNKS, lambda q: run(1, n, lambda k: symbol_copy(g, q, k).start()))

    def decode(g, q):
        run(1, n, lambda k: symbol_copy(g, q, k).wait_recv())
        slots = slice(g * half, (g + 1) * half)

        def tile(s, carry):
            t = q * per + s
            for h in range(TILE // LANES):
                side = slice(h * LANES, (h + 1) * LANES)
                total = jnp.zeros((half, LANES), jnp.float32)
                for source in range(n):
                    value = symr[t, source, slots, side].astype(jnp.float32)
                    value = jnp.clip(value, 0.0, float(count - 1))
                    if source % 2:
                        total = total + piecewise(value, whole, starts, gaps)
                    else:
                        at = value.astype(jnp.int32)
                        total = total + (lookup(start, at) + lookup(delta, at) * value)
                sums[t, slots, side] = total * slot_scale[slots]
            return carry

        lax.fori_loop(0, per, tile, 0)

    def gather_copy(g, c):
        peer = lax.rem(chip + c, chips) * 2 + core
        slots = pl.ds(g * half, half)
        return pltpu.make_async_remote_copy(
            src_ref=pr.at[slots], dst_ref=gall.at[me, slots], send_sem=gs_sem.at[g, c], recv_sem=gr_sem.at[g, c],
            device_id={"dp": peer}, device_id_type=MESH,
        )

    def relay_copy(g, c):
        source = lax.rem(chip + chips - c, chips) * 2 + core
        slots = pl.ds(g * half, half)
        return pltpu.make_async_remote_copy(
            src_ref=gall.at[source, slots], dst_ref=gall.at[source, slots],
            send_sem=rs_sem.at[g, c], recv_sem=rr_sem.at[g, c],
            device_id={"dp": partner}, device_id_type=MESH,
        )

    def own_relay(g):
        slots = pl.ds(g * half, half)
        return pltpu.make_async_remote_copy(
            src_ref=pr.at[slots], dst_ref=gall.at[me, slots], send_sem=rs_sem.at[g, 0], recv_sem=rr_sem.at[g, 0],
            device_id={"dp": partner}, device_id_type=MESH,
        )

    for side in sides:
        side.wait()
    for g in range(groups):
        run(0, CHUNKS, functools.partial(decode, g))
        slots = slice(g * half, (g + 1) * half)
        grads = transform([sums[c, slots] for c in range(tiles)], hmat[...])
        for c in range(tiles):
            cut = slice(c * TILE, (c + 1) * TILE)
            grad = grads[c] * flip[:, cut]
            master = mst[slots, cut]
            first = first_decay * fm[slots, cut] + (1.0 - first_decay) * grad
            second = second_decay * sm[slots, cut] + (1.0 - second_decay) * grad * grad
            fresh = master - learning_rate * (first / (jnp.sqrt(second) + adam_epsilon) + weight_decay * master)
            uf[slots, cut] = first
            us[slots, cut] = second
            um[slots, cut] = fresh
            pr[slots, cut] = fresh.astype(jnp.bfloat16)
        run(1, chips, lambda c: gather_copy(g, c).start())
        own_relay(g).start()
    outs = [
        pltpu.make_async_copy(src, dst, side_sem.at[3 + i])
        for i, (src, dst) in enumerate(((um, um_hbm), (uf, uf_hbm), (us, us_hbm), (pr, gall.at[me])))
    ]
    for out in outs:
        out.start()

    for g in range(groups):
        def relay(c):
            gather_copy(g, c).wait_recv()
            relay_copy(g, c).start()

        run(1, chips, relay)
    for g in range(groups):
        own_relay(g).wait()
        run(1, chips, lambda c: relay_copy(g, c).wait())
        run(1, chips, lambda c: gather_copy(g, c).wait_send())
        run(0, CHUNKS, lambda q: run(1, n, lambda k: symbol_copy(g, q, k).wait_send()))
    run(1, n, lambda k: peak_copy(k).wait_send())
    for out in outs:
        out.wait()


def spread_kernel(layout_ref, gall_ref, um_in, uf_in, us_in, um_out, uf_out, us_out, out_ref):
    blocks = layout_ref.shape[1]
    rows = lax.broadcasted_iota(jnp.int32, (blocks, blocks), 0)
    table = (rows == layout_ref[...]).astype(jnp.float32).astype(jnp.bfloat16)
    out_ref[...] = jnp.dot(table, gall_ref[...], preferred_element_type=jnp.float32).astype(jnp.bfloat16)
    um_out[...] = um_in[...]
    uf_out[...] = uf_in[...]
    us_out[...] = us_in[...]


def local(n, gradient, dither, sign_bits, levels, layout, master, first_moment, second_moment):
    blocks, size = gradient.shape[2:]
    own = blocks // n
    tiles = size // TILE
    row_chunks = 8
    groups = slot_groups(own)
    f32, bf16 = jnp.float32, jnp.bfloat16
    hbm = pl.BlockSpec(memory_space=pl.ANY)
    vmem = pl.BlockSpec(memory_space=pltpu.VMEM)
    dma = pltpu.SemaphoreType.DMA
    layout_row = layout.reshape(1, blocks)
    shard = jax.ShapeDtypeStruct((own, size), f32)
    um, uf, us, gall = pl.pallas_call(
        functools.partial(step_kernel, n),
        out_shape=(shard, shard, shard, jax.ShapeDtypeStruct((n, own, size), bf16)),
        in_specs=[hbm, hbm, vmem, pl.BlockSpec(memory_space=pltpu.SMEM), vmem, hbm, hbm, hbm],
        out_specs=(hbm, hbm, hbm, hbm),
        scratch_shapes=[
            pltpu.VMEM((blocks, size), f32),
            pltpu.VMEM((tiles, blocks, TILE), jnp.int32),
            pltpu.VMEM((tiles, blocks, TILE), f32),
            pltpu.VMEM((blocks, blocks), f32),
            pltpu.VMEM((TILE, TILE), bf16),
            pltpu.VMEM((1, size), f32),
            pltpu.VMEM((blocks, LANES), f32),
            pltpu.VMEM((8, blocks), f32),
            pltpu.VMEM((n, 8, blocks), f32),
            pltpu.VMEM((blocks, TILE), bf16),
            pltpu.VMEM((tiles, n, own, TILE), bf16),
            pltpu.VMEM((tiles, n, own, TILE), bf16),
            pltpu.VMEM((tiles, own, TILE), f32),
            *[pltpu.VMEM((own, size), f32)] * 6,
            pltpu.VMEM((own, size), bf16),
            dma((row_chunks,)),
            dma((tiles,)),
            dma((7,)),
            dma((n,)),
            dma((n,)),
            dma((groups, CHUNKS, n)),
            dma((groups, CHUNKS, n)),
            *[dma((groups, n // 2))] * 4,
        ],
        compiler_params=pltpu.CompilerParams(
            collective_id=0, has_side_effects=True, vmem_limit_bytes=VMEM_LIMIT
        ),
    )(
        gradient[0, 0], dither[0, 0], sign_bits.reshape(1, size), levels, layout_row,
        master[0], first_moment[0], second_moment[0],
    )
    width = size // 8
    wide = pl.BlockSpec((blocks, width), lambda i: (0, i))
    narrow = pl.BlockSpec((own, width), lambda i: (0, i))
    um, uf, us, parameters = pl.pallas_call(
        spread_kernel,
        grid=(8,),
        out_shape=(shard, shard, shard, jax.ShapeDtypeStruct((blocks, size), bf16)),
        in_specs=[pl.BlockSpec((1, blocks), lambda i: (0, 0)), wide, narrow, narrow, narrow],
        out_specs=(narrow, narrow, narrow, wide),
    )(layout_row, gall.reshape(blocks, size), um, uf, us)
    return um[None], uf[None], us[None], parameters[None]


def solution(mesh):
    slots = P("section", "dp", None)
    streams = P("section", "dp", None, None)
    return jax.shard_map(
        functools.partial(local, mesh.shape["dp"]),
        mesh=mesh,
        in_specs=(streams, streams, P(), P(), P(), slots, slots, slots),
        out_specs=(slots, slots, slots, P("section", None, None)),
        check_vma=False,
    )
```

```python
import functools
import math

import jax
import jax.numpy as jnp
from jax import lax
from jax.experimental import pallas as pl
from jax.experimental.pallas import tpu as pltpu
from jax.sharding import PartitionSpec as P

MESH = pl.DeviceIdType.MESH
adam_epsilon = 1e-08
learning_rate = 0.02
weight_decay = 0.1
first_decay = 0.9
second_decay = 0.95
dither_steps = 256.0
CHUNKS = 8
LANES = 128
TILE = 256
VMEM_LIMIT = 60 * 1024 * 1024


def hadamard(edge, scale):
    rows = lax.broadcasted_iota(jnp.int32, (edge, edge), 0)
    columns = lax.broadcasted_iota(jnp.int32, (edge, edge), 1)
    common = rows & columns
    parity = jnp.zeros((edge, edge), jnp.int32)
    for bit in range(edge.bit_length() - 1):
        parity = parity + ((common >> bit) & 1)
    return ((1 - 2 * (parity & 1)).astype(jnp.float32) * scale).astype(jnp.bfloat16)


def exact_dot(x, table):
    high = x.astype(jnp.bfloat16)
    rest = x - high.astype(jnp.float32)
    middle = rest.astype(jnp.bfloat16)
    low = (rest - middle.astype(jnp.float32)).astype(jnp.bfloat16)
    dot = functools.partial(jnp.dot, preferred_element_type=jnp.float32)
    return dot(high, table) + (dot(middle, table) + dot(low, table))


def butterflies(pieces):
    pieces = list(pieces)
    step = 1
    while step < len(pieces):
        for i in range(len(pieces)):
            if not i & step:
                a, b = pieces[i], pieces[i + step]
                pieces[i], pieces[i + step] = a + b, a - b
        step *= 2
    return pieces


def transform(pieces, table):
    rows = pieces[0].shape[0]
    turned = exact_dot(jnp.concatenate(pieces, axis=0), table)
    return butterflies([turned[c * rows : (c + 1) * rows] for c in range(len(pieces))])


def lookup(table, index):
    return jnp.take_along_axis(
        jnp.broadcast_to(table, index.shape), index, axis=1, mode="promise_in_bounds"
    )


def piecewise(value, spots, bases, slopes):
    base = jnp.full(value.shape, bases[0], jnp.float32)
    slope = jnp.full(value.shape, slopes[0], jnp.float32)
    for spot, next_base, next_slope in zip(spots, bases[1:], slopes[1:]):
        past = value >= spot
        base = jnp.where(past, next_base, base)
        slope = jnp.where(past, next_slope, slope)
    return base + slope * value


def slot_groups(own):
    return 2 if own % 32 == 0 else 1


def level_rows(levels_ref, count):
    lane = lax.broadcasted_iota(jnp.int32, (1, LANES), 1)
    here = jnp.zeros((1, LANES), jnp.float32)
    after = jnp.zeros((1, LANES), jnp.float32)
    for k in range(count):
        here = jnp.where(lane == k, levels_ref[k], here)
        after = jnp.where(lane == k, levels_ref[min(k + 1, count - 1)], after)
    return lane, here, after


def step_kernel(
    n, grad_hbm, dith_hbm, sign_ref, levels_ref, layout_ref, mst_hbm, fm_hbm, sm_hbm,
    um_hbm, uf_hbm, us_hbm, gall,
    x, dith, rot, pmat, hmat, flip, peaks, pk_send, pk_recv, symt, sym, symr, sums,
    mst, fm, sm, um, uf, us, pr,
    load_sem, dith_sem, side_sem, pks_sem, pkr_sem, as_sem, ar_sem, gs_sem, gr_sem, rs_sem, rr_sem,
):
    me = lax.axis_index("dp")
    blocks, size = x.shape
    own = blocks // n
    tiles = size // TILE
    per = tiles // CHUNKS
    rows = blocks // load_sem.shape[0]
    chips = n // 2
    chip, core = me // 2, lax.rem(me, 2)
    partner = chip * 2 + 1 - core
    count = levels_ref.shape[0]
    groups = slot_groups(own)
    half = own // groups

    def load(i):
        part = pl.ds(pl.multiple_of(i * rows, rows), rows)
        return pltpu.make_async_copy(grad_hbm.at[part], x.at[part], load_sem.at[i])

    for i in range(blocks // rows):
        load(i).start()

    def load_dither(t):
        return pltpu.make_async_copy(
            dith_hbm.at[:, t * TILE : (t + 1) * TILE], dith.at[t], dith_sem.at[t]
        )

    for t in range(tiles):
        load_dither(t).start()
    sides = [
        pltpu.make_async_copy(src, dst, side_sem.at[i])
        for i, (src, dst) in enumerate(((mst_hbm, mst), (fm_hbm, fm), (sm_hbm, sm)))
    ]
    for side in sides:
        side.start()

    barrier = pltpu.get_barrier_semaphore()

    def greet(k, carry):
        pl.semaphore_signal(barrier, inc=1, device_id={"dp": lax.rem(me + k, n)}, device_id_type=MESH)
        return carry

    lax.fori_loop(1, n, greet, 0)

    flip[...] = (1 - 2 * sign_ref[...]).astype(jnp.float32)
    hmat[...] = hadamard(TILE, 1.0 / math.isqrt(size))
    block_row = lax.broadcasted_iota(jnp.int32, (blocks, blocks), 0)
    block_col = lax.broadcasted_iota(jnp.int32, (blocks, blocks), 1)
    turned_p = (block_row == layout_ref[...]).astype(jnp.float32)
    pmat[...] = turned_p.T

    @pl.loop(0, blocks // rows)
    def _(i):
        load(i).wait()
        part = pl.ds(pl.multiple_of(i * rows, rows), rows)
        pieces = [x[part, c * TILE : (c + 1) * TILE] * flip[:, c * TILE : (c + 1) * TILE] for c in range(tiles)]
        pieces = transform(pieces, hmat[...])
        top = jnp.abs(pieces[0])
        for c in range(tiles):
            rot[c, part] = pieces[c]
            top = jnp.maximum(top, jnp.abs(pieces[c]))
        peaks[part] = jnp.broadcast_to(jnp.max(top, axis=1, keepdims=True), (rows, LANES))

    eye = block_row == block_col
    peak_row = jnp.max(jnp.where(eye, peaks[:, :1], 0.0), axis=0, keepdims=True)
    pk_send[...] = jnp.broadcast_to(peak_row, pk_send.shape)
    pl.semaphore_wait(barrier, n - 1)

    def peak_copy(k):
        return pltpu.make_async_remote_copy(
            src_ref=pk_send, dst_ref=pk_recv.at[k], send_sem=pks_sem.at[k], recv_sem=pkr_sem.at[k],
            device_id={"dp": lax.rem(me + k, n)}, device_id_type=MESH,
        )

    def run(first, last, do):
        def body(k, carry):
            do(k)
            return carry
        lax.fori_loop(first, last, body, 0)

    run(1, n, lambda k: peak_copy(k).start())

    lane, here, after = level_rows(levels_ref, count)
    inside = lane < count - 1
    delta = jnp.where(inside, after - here, 0.0)
    start = jnp.where(inside, here - delta * lane.astype(jnp.float32), here)
    spots = [levels_ref[k] for k in range(1, count - 1)]
    gaps = [levels_ref[k + 1] - levels_ref[k] for k in range(count - 1)]
    slopes = [1.0 / gap for gap in gaps]
    bases = [float(k) - levels_ref[k] * slopes[k] for k in range(count - 1)]
    whole = [float(k) for k in range(1, count - 1)]
    starts = [levels_ref[k] - gaps[k] * float(k) for k in range(count - 1)]

    run(1, n, lambda k: peak_copy(k).wait_recv())
    best = pk_send[...]
    for k in range(1, n):
        best = jnp.maximum(best, pk_recv[k])
    scale_row = best[:1] + 1e-06
    scale_col = jnp.max(jnp.where(eye, scale_row, 0.0), axis=1, keepdims=True)
    peaks[...] = jnp.broadcast_to(1.0 / scale_col, peaks.shape)
    mine = pl.ds(pl.multiple_of(me * own, own), own)
    slot_scale = jnp.max(pmat[mine] * scale_row, axis=1, keepdims=True)
    perm = pmat[...].astype(jnp.bfloat16)

    def symbol_copy(g, q, k):
        peer = lax.rem(me + k, n)
        part = pl.ds(q * per, per)
        slots = pl.ds(g * half, half)
        return pltpu.make_async_remote_copy(
            src_ref=sym.at[part, peer, slots], dst_ref=symr.at[part, me, slots],
            send_sem=as_sem.at[g, q, k], recv_sem=ar_sem.at[g, q, k],
            device_id={"dp": peer}, device_id_type=MESH,
        )

    group = 32
    for t in range(tiles):
        load_dither(t).wait()

    def encode(q):
        def tile(s, carry):
            t = q * per + s
            for r in range(blocks // group):
                part = slice(r * group, (r + 1) * group)
                inverse = peaks[part]
                for h in range(TILE // LANES):
                    side = slice(h * LANES, (h + 1) * LANES)
                    ratio = rot[t, part, side] * inverse
                    relaxed = piecewise(ratio, spots, bases, slopes)
                    offset = dith[t, part, side].astype(jnp.float32) * (1.0 / dither_steps) + (0.5 / dither_steps - 0.5)
                    symt[part, side] = (relaxed + offset).astype(jnp.bfloat16)
            moved = jnp.dot(perm, symt[...], preferred_element_type=jnp.float32).astype(jnp.bfloat16)
            sym[t] = moved.reshape(n, own, TILE)
            symr[t, me] = sym[t, me]
            return carry

        lax.fori_loop(0, per, tile, 0)
        run(1, n, lambda k: symbol_copy(0, q, k).start())

    run(0, CHUNKS, encode)
    for g in range(1, groups):
        run(0, CHUNKS, lambda q: run(1, n, lambda k: symbol_copy(g, q, k).start()))

    def decode(g, q):
        run(1, n, lambda k: symbol_copy(g, q, k).wait_recv())
        slots = slice(g * half, (g + 1) * half)

        def tile(s, carry):
            t = q * per + s
            for h in range(TILE // LANES):
                side = slice(h * LANES, (h + 1) * LANES)
                total = jnp.zeros((half, LANES), jnp.float32)
                for source in range(n):
                    value = symr[t, source, slots, side].astype(jnp.float32)
                    value = jnp.clip(value, 0.0, float(count - 1))
                    if source % 2:
                        total = total + piecewise(value, whole, starts, gaps)
                    else:
                        at = value.astype(jnp.int32)
                        total = total + (lookup(start, at) + lookup(delta, at) * value)
                sums[t, slots, side] = total * slot_scale[slots]
            return carry

        lax.fori_loop(0, per, tile, 0)

    def gather_copy(g, c):
        peer = lax.rem(chip + c, chips) * 2 + core
        slots = pl.ds(g * half, half)
        return pltpu.make_async_remote_copy(
            src_ref=pr.at[slots], dst_ref=gall.at[me, slots], send_sem=gs_sem.at[g, c], recv_sem=gr_sem.at[g, c],
            device_id={"dp": peer}, device_id_type=MESH,
        )

    def relay_copy(g, c):
        source = lax.rem(chip + chips - c, chips) * 2 + core
        slots = pl.ds(g * half, half)
        return pltpu.make_async_remote_copy(
            src_ref=gall.at[source, slots], dst_ref=gall.at[source, slots],
            send_sem=rs_sem.at[g, c], recv_sem=rr_sem.at[g, c],
            device_id={"dp": partner}, device_id_type=MESH,
        )

    def own_relay(g):
        slots = pl.ds(g * half, half)
        return pltpu.make_async_remote_copy(
            src_ref=pr.at[slots], dst_ref=gall.at[me, slots], send_sem=rs_sem.at[g, 0], recv_sem=rr_sem.at[g, 0],
            device_id={"dp": partner}, device_id_type=MESH,
        )

    square = chips == 4
    near = chip + 1 - 2 * lax.rem(chip, 2)
    across = lax.rem(chip + 2, 4)
    corner = lax.rem(near + 2, 4)
    left, right, full = (0, size // 2), (size // 2, size // 2), (0, size)

    def shard_copy(g, kind, source, columns, to_chip, send, recv):
        at = gall.at[source, pl.ds(g * half, half), pl.ds(*columns)]
        own_part = pr.at[pl.ds(g * half, half), pl.ds(*columns)]
        return pltpu.make_async_remote_copy(
            src_ref=own_part if source is me else at, dst_ref=at,
            send_sem=send.at[g, kind], recv_sem=recv.at[g, kind],
            device_id={"dp": to_chip}, device_id_type=MESH,
        )

    def square_copies(g):
        to_near, to_across = near * 2 + core, across * 2 + core
        hops = [
            shard_copy(g, 0, me, left, to_near, gs_sem, gr_sem),
            shard_copy(g, 1, me, right, to_across, gs_sem, gr_sem),
            shard_copy(g, 2, me, right, to_near, gs_sem, gr_sem),
            shard_copy(g, 3, me, left, to_across, gs_sem, gr_sem),
            shard_copy(g, 4, to_near, left, to_across, gs_sem, gr_sem),
            shard_copy(g, 5, to_across, right, to_near, gs_sem, gr_sem),
        ]
        shares = [
            shard_copy(g, i, source, full, partner, rs_sem, rr_sem)
            for i, source in enumerate((me, to_near, to_across, corner * 2 + core))
        ]
        return hops, shares

    for side in sides:
        side.wait()
    for g in range(groups):
        run(0, CHUNKS, functools.partial(decode, g))
        slots = slice(g * half, (g + 1) * half)
        grads = transform([sums[c, slots] for c in range(tiles)], hmat[...])
        for c in range(tiles):
            cut = slice(c * TILE, (c + 1) * TILE)
            grad = grads[c] * flip[:, cut]
            master = mst[slots, cut]
            first = first_decay * fm[slots, cut] + (1.0 - first_decay) * grad
            second = second_decay * sm[slots, cut] + (1.0 - second_decay) * grad * grad
            fresh = master - learning_rate * (first / (jnp.sqrt(second) + adam_epsilon) + weight_decay * master)
            uf[slots, cut] = first
            us[slots, cut] = second
            um[slots, cut] = fresh
            pr[slots, cut] = fresh.astype(jnp.bfloat16)
        if square:
            hops, shares = square_copies(g)
            for hop in hops[:4]:
                hop.start()
            shares[0].start()
        else:
            run(1, chips, lambda c: gather_copy(g, c).start())
            own_relay(g).start()
    outs = [
        pltpu.make_async_copy(src, dst, side_sem.at[3 + i])
        for i, (src, dst) in enumerate(((um, um_hbm), (uf, uf_hbm), (us, us_hbm), (pr, gall.at[me])))
    ]
    for out in outs:
        out.start()

    for g in range(groups):
        def relay(c):
            gather_copy(g, c).wait_recv()
            relay_copy(g, c).start()

        if square:
            hops, shares = square_copies(g)
            hops[0].wait_recv()
            hops[4].start()
            hops[1].wait_recv()
            hops[5].start()
        else:
            run(1, chips, relay)
    if square:
        for g in range(groups):
            hops, shares = square_copies(g)
            hops[2].wait_recv()
            shares[1].start()
            hops[3].wait_recv()
            shares[2].start()
        for g in range(groups):
            hops, shares = square_copies(g)
            hops[4].wait_recv()
            hops[5].wait_recv()
            shares[3].start()
    for g in range(groups):
        if square:
            hops, shares = square_copies(g)
            for share in shares:
                share.wait()
            for hop in hops:
                hop.wait_send()
        else:
            own_relay(g).wait()
            run(1, chips, lambda c: relay_copy(g, c).wait())
            run(1, chips, lambda c: gather_copy(g, c).wait_send())
        run(0, CHUNKS, lambda q: run(1, n, lambda k: symbol_copy(g, q, k).wait_send()))
    run(1, n, lambda k: peak_copy(k).wait_send())
    for out in outs:
        out.wait()


def spread_kernel(layout_ref, gall_ref, um_in, uf_in, us_in, um_out, uf_out, us_out, out_ref):
    blocks = layout_ref.shape[1]
    rows = lax.broadcasted_iota(jnp.int32, (blocks, blocks), 0)
    table = (rows == layout_ref[...]).astype(jnp.float32).astype(jnp.bfloat16)
    out_ref[...] = jnp.dot(table, gall_ref[...], preferred_element_type=jnp.float32).astype(jnp.bfloat16)
    um_out[...] = um_in[...]
    uf_out[...] = uf_in[...]
    us_out[...] = us_in[...]


def local(n, gradient, dither, sign_bits, levels, layout, master, first_moment, second_moment):
    blocks, size = gradient.shape[2:]
    own = blocks // n
    tiles = size // TILE
    row_chunks = 8
    groups = slot_groups(own)
    f32, bf16 = jnp.float32, jnp.bfloat16
    hbm = pl.BlockSpec(memory_space=pl.ANY)
    vmem = pl.BlockSpec(memory_space=pltpu.VMEM)
    dma = pltpu.SemaphoreType.DMA
    layout_row = layout.reshape(1, blocks)
    shard = jax.ShapeDtypeStruct((own, size), f32)
    um, uf, us, gall = pl.pallas_call(
        functools.partial(step_kernel, n),
        out_shape=(shard, shard, shard, jax.ShapeDtypeStruct((n, own, size), bf16)),
        in_specs=[hbm, hbm, vmem, pl.BlockSpec(memory_space=pltpu.SMEM), vmem, hbm, hbm, hbm],
        out_specs=(hbm, hbm, hbm, hbm),
        scratch_shapes=[
            pltpu.VMEM((blocks, size), f32),
            pltpu.VMEM((tiles, blocks, TILE), jnp.int32),
            pltpu.VMEM((tiles, blocks, TILE), f32),
            pltpu.VMEM((blocks, blocks), f32),
            pltpu.VMEM((TILE, TILE), bf16),
            pltpu.VMEM((1, size), f32),
            pltpu.VMEM((blocks, LANES), f32),
            pltpu.VMEM((8, blocks), f32),
            pltpu.VMEM((n, 8, blocks), f32),
            pltpu.VMEM((blocks, TILE), bf16),
            pltpu.VMEM((tiles, n, own, TILE), bf16),
            pltpu.VMEM((tiles, n, own, TILE), bf16),
            pltpu.VMEM((tiles, own, TILE), f32),
            *[pltpu.VMEM((own, size), f32)] * 6,
            pltpu.VMEM((own, size), bf16),
            dma((row_chunks,)),
            dma((tiles,)),
            dma((7,)),
            dma((n,)),
            dma((n,)),
            dma((groups, CHUNKS, n)),
            dma((groups, CHUNKS, n)),
            *[dma((groups, max(6, n // 2)))] * 4,
        ],
        compiler_params=pltpu.CompilerParams(
            collective_id=0, has_side_effects=True, vmem_limit_bytes=VMEM_LIMIT
        ),
    )(
        gradient[0, 0], dither[0, 0], sign_bits.reshape(1, size), levels, layout_row,
        master[0], first_moment[0], second_moment[0],
    )
    width = size // 8
    wide = pl.BlockSpec((blocks, width), lambda i: (0, i))
    narrow = pl.BlockSpec((own, width), lambda i: (0, i))
    um, uf, us, parameters = pl.pallas_call(
        spread_kernel,
        grid=(8,),
        out_shape=(shard, shard, shard, jax.ShapeDtypeStruct((blocks, size), bf16)),
        in_specs=[pl.BlockSpec((1, blocks), lambda i: (0, 0)), wide, narrow, narrow, narrow],
        out_specs=(narrow, narrow, narrow, wide),
    )(layout_row, gall.reshape(blocks, size), um, uf, us)
    return um[None], uf[None], us[None], parameters[None]


def solution(mesh):
    slots = P("section", "dp", None)
    streams = P("section", "dp", None, None)
    return jax.shard_map(
        functools.partial(local, mesh.shape["dp"]),
        mesh=mesh,
        in_specs=(streams, streams, P(), P(), P(), slots, slots, slots),
        out_specs=(slots, slots, slots, P("section", None, None)),
        check_vma=False,
    )
```

```python
import functools
import math

import jax
import jax.numpy as jnp
from jax import lax
from jax.experimental import pallas as pl
from jax.experimental.pallas import tpu as pltpu
from jax.sharding import PartitionSpec as P

MESH = pl.DeviceIdType.MESH
adam_epsilon = 1e-08
learning_rate = 0.02
weight_decay = 0.1
first_decay = 0.9
second_decay = 0.95
dither_steps = 256.0
CHUNKS = 8
LANES = 128
TILE = 256
VMEM_LIMIT = 60 * 1024 * 1024


def hadamard(edge, scale):
    rows = lax.broadcasted_iota(jnp.int32, (edge, edge), 0)
    columns = lax.broadcasted_iota(jnp.int32, (edge, edge), 1)
    common = rows & columns
    parity = jnp.zeros((edge, edge), jnp.int32)
    for bit in range(edge.bit_length() - 1):
        parity = parity + ((common >> bit) & 1)
    return ((1 - 2 * (parity & 1)).astype(jnp.float32) * scale).astype(jnp.bfloat16)


def exact_dot(x, table):
    high = x.astype(jnp.bfloat16)
    rest = x - high.astype(jnp.float32)
    middle = rest.astype(jnp.bfloat16)
    low = (rest - middle.astype(jnp.float32)).astype(jnp.bfloat16)
    dot = functools.partial(jnp.dot, preferred_element_type=jnp.float32)
    return dot(high, table) + (dot(middle, table) + dot(low, table))


def butterflies(pieces):
    pieces = list(pieces)
    step = 1
    while step < len(pieces):
        for i in range(len(pieces)):
            if not i & step:
                a, b = pieces[i], pieces[i + step]
                pieces[i], pieces[i + step] = a + b, a - b
        step *= 2
    return pieces


def transform(pieces, table):
    rows = pieces[0].shape[0]
    turned = exact_dot(jnp.concatenate(pieces, axis=0), table)
    return butterflies([turned[c * rows : (c + 1) * rows] for c in range(len(pieces))])


def lookup(table, index):
    return jnp.take_along_axis(
        jnp.broadcast_to(table, index.shape), index, axis=1, mode="promise_in_bounds"
    )


def piecewise(value, spots, bases, slopes):
    base = jnp.full(value.shape, bases[0], jnp.float32)
    slope = jnp.full(value.shape, slopes[0], jnp.float32)
    for spot, next_base, next_slope in zip(spots, bases[1:], slopes[1:]):
        past = value >= spot
        base = jnp.where(past, next_base, base)
        slope = jnp.where(past, next_slope, slope)
    return base + slope * value


def slot_groups(own):
    return 2 if own % 32 == 0 else 1


def level_rows(levels_ref, count):
    lane = lax.broadcasted_iota(jnp.int32, (1, LANES), 1)
    here = jnp.zeros((1, LANES), jnp.float32)
    after = jnp.zeros((1, LANES), jnp.float32)
    for k in range(count):
        here = jnp.where(lane == k, levels_ref[k], here)
        after = jnp.where(lane == k, levels_ref[min(k + 1, count - 1)], after)
    return lane, here, after


def step_kernel(
    n, grad_hbm, dith_hbm, sign_ref, levels_ref, layout_ref, mst_hbm, fm_hbm, sm_hbm,
    um_hbm, uf_hbm, us_hbm, gall,
    x, dith, rot, pmat, hmat, flip, peaks, pk_send, pk_recv, symt, sym, symr, sums,
    mst, fm, sm, um, uf, us, pr,
    load_sem, dith_sem, side_sem, pks_sem, pkr_sem, as_sem, ar_sem, gs_sem, gr_sem, rs_sem, rr_sem,
):
    me = lax.axis_index("dp")
    blocks, size = x.shape
    own = blocks // n
    tiles = size // TILE
    per = tiles // CHUNKS
    rows = blocks // load_sem.shape[0]
    chips = n // 2
    chip, core = me // 2, lax.rem(me, 2)
    partner = chip * 2 + 1 - core
    count = levels_ref.shape[0]
    groups = slot_groups(own)
    half = own // groups

    def load(i):
        part = pl.ds(pl.multiple_of(i * rows, rows), rows)
        return pltpu.make_async_copy(grad_hbm.at[part], x.at[part], load_sem.at[i])

    for i in range(blocks // rows):
        load(i).start()

    def load_dither(t):
        return pltpu.make_async_copy(
            dith_hbm.at[:, t * TILE : (t + 1) * TILE], dith.at[t], dith_sem.at[t]
        )

    for t in range(tiles):
        load_dither(t).start()
    sides = [
        pltpu.make_async_copy(src, dst, side_sem.at[i])
        for i, (src, dst) in enumerate(((mst_hbm, mst), (fm_hbm, fm), (sm_hbm, sm)))
    ]
    for side in sides:
        side.start()

    barrier = pltpu.get_barrier_semaphore()

    def greet(k, carry):
        pl.semaphore_signal(barrier, inc=1, device_id={"dp": lax.rem(me + k, n)}, device_id_type=MESH)
        return carry

    lax.fori_loop(1, n, greet, 0)

    flip[...] = (1 - 2 * sign_ref[...]).astype(jnp.float32)
    hmat[...] = hadamard(TILE, 1.0 / math.isqrt(size))
    block_row = lax.broadcasted_iota(jnp.int32, (blocks, blocks), 0)
    block_col = lax.broadcasted_iota(jnp.int32, (blocks, blocks), 1)
    turned_p = (block_row == layout_ref[...]).astype(jnp.float32)
    pmat[...] = turned_p.T

    @pl.loop(0, blocks // rows)
    def _(i):
        load(i).wait()
        part = pl.ds(pl.multiple_of(i * rows, rows), rows)
        pieces = [x[part, c * TILE : (c + 1) * TILE] * flip[:, c * TILE : (c + 1) * TILE] for c in range(tiles)]
        pieces = transform(pieces, hmat[...])
        top = jnp.abs(pieces[0])
        for c in range(tiles):
            rot[c, part] = pieces[c]
            top = jnp.maximum(top, jnp.abs(pieces[c]))
        peaks[part] = jnp.broadcast_to(jnp.max(top, axis=1, keepdims=True), (rows, LANES))

    eye = block_row == block_col
    peak_row = jnp.max(jnp.where(eye, peaks[:, :1], 0.0), axis=0, keepdims=True)
    pk_send[...] = jnp.broadcast_to(peak_row, pk_send.shape)
    pl.semaphore_wait(barrier, n - 1)

    def peak_copy(k):
        return pltpu.make_async_remote_copy(
            src_ref=pk_send, dst_ref=pk_recv.at[k], send_sem=pks_sem.at[k], recv_sem=pkr_sem.at[k],
            device_id={"dp": lax.rem(me + k, n)}, device_id_type=MESH,
        )

    def run(first, last, do):
        def body(k, carry):
            do(k)
            return carry
        lax.fori_loop(first, last, body, 0)

    run(1, n, lambda k: peak_copy(k).start())

    lane, here, after = level_rows(levels_ref, count)
    inside = lane < count - 1
    delta = jnp.where(inside, after - here, 0.0)
    start = jnp.where(inside, here - delta * lane.astype(jnp.float32), here)
    spots = [levels_ref[k] for k in range(1, count - 1)]
    gaps = [levels_ref[k + 1] - levels_ref[k] for k in range(count - 1)]
    slopes = [1.0 / gap for gap in gaps]
    bases = [float(k) - levels_ref[k] * slopes[k] for k in range(count - 1)]
    whole = [float(k) for k in range(1, count - 1)]
    starts = [levels_ref[k] - gaps[k] * float(k) for k in range(count - 1)]

    run(1, n, lambda k: peak_copy(k).wait_recv())
    best = pk_send[...]
    for k in range(1, n):
        best = jnp.maximum(best, pk_recv[k])
    scale_row = best[:1] + 1e-06
    scale_col = jnp.max(jnp.where(eye, scale_row, 0.0), axis=1, keepdims=True)
    peaks[...] = jnp.broadcast_to(1.0 / scale_col, peaks.shape)
    mine = pl.ds(pl.multiple_of(me * own, own), own)
    slot_scale = jnp.max(pmat[mine] * scale_row, axis=1, keepdims=True)
    perm = pmat[...].astype(jnp.bfloat16)

    def symbol_copy(g, q, k):
        peer = lax.rem(me + k, n)
        part = pl.ds(q * per, per)
        slots = pl.ds(g * half, half)
        return pltpu.make_async_remote_copy(
            src_ref=sym.at[part, peer, slots], dst_ref=symr.at[part, me, slots],
            send_sem=as_sem.at[g, q, k], recv_sem=ar_sem.at[g, q, k],
            device_id={"dp": peer}, device_id_type=MESH,
        )

    group = 32
    for t in range(tiles):
        load_dither(t).wait()

    def encode(q):
        def tile(s, carry):
            t = q * per + s
            for r in range(blocks // group):
                part = slice(r * group, (r + 1) * group)
                inverse = peaks[part]
                for h in range(TILE // LANES):
                    side = slice(h * LANES, (h + 1) * LANES)
                    ratio = rot[t, part, side] * inverse
                    relaxed = piecewise(ratio, spots, bases, slopes)
                    offset = dith[t, part, side].astype(jnp.float32) * (1.0 / dither_steps) + (0.5 / dither_steps - 0.5)
                    symt[part, side] = (relaxed + offset).astype(jnp.bfloat16)
            moved = jnp.dot(perm, symt[...], preferred_element_type=jnp.float32).astype(jnp.bfloat16)
            sym[t] = moved.reshape(n, own, TILE)
            symr[t, me] = sym[t, me]
            return carry

        lax.fori_loop(0, per, tile, 0)
        run(1, n, lambda k: symbol_copy(0, q, k).start())

    run(0, CHUNKS, encode)
    for g in range(1, groups):
        run(0, CHUNKS, lambda q: run(1, n, lambda k: symbol_copy(g, q, k).start()))

    def decode(g, q):
        run(1, n, lambda k: symbol_copy(g, q, k).wait_recv())
        slots = slice(g * half, (g + 1) * half)

        def tile(s, carry):
            t = q * per + s
            for h in range(TILE // LANES):
                side = slice(h * LANES, (h + 1) * LANES)
                total = jnp.zeros((half, LANES), jnp.float32)
                for source in range(n):
                    value = symr[t, source, slots, side].astype(jnp.float32)
                    value = jnp.clip(value, 0.0, float(count - 1))
                    if source % 2:
                        total = total + piecewise(value, whole, starts, gaps)
                    else:
                        at = value.astype(jnp.int32)
                        total = total + (lookup(start, at) + lookup(delta, at) * value)
                sums[t, slots, side] = total * slot_scale[slots]
            return carry

        lax.fori_loop(0, per, tile, 0)

    def gather_copy(g, c):
        peer = lax.rem(chip + c, chips) * 2 + core
        slots = pl.ds(g * half, half)
        return pltpu.make_async_remote_copy(
            src_ref=pr.at[slots], dst_ref=gall.at[me, slots], send_sem=gs_sem.at[g, c], recv_sem=gr_sem.at[g, c],
            device_id={"dp": peer}, device_id_type=MESH,
        )

    def relay_copy(g, c):
        source = lax.rem(chip + chips - c, chips) * 2 + core
        slots = pl.ds(g * half, half)
        return pltpu.make_async_remote_copy(
            src_ref=gall.at[source, slots], dst_ref=gall.at[source, slots],
            send_sem=rs_sem.at[g, c], recv_sem=rr_sem.at[g, c],
            device_id={"dp": partner}, device_id_type=MESH,
        )

    def own_relay(g):
        slots = pl.ds(g * half, half)
        return pltpu.make_async_remote_copy(
            src_ref=pr.at[slots], dst_ref=gall.at[me, slots], send_sem=rs_sem.at[g, 0], recv_sem=rr_sem.at[g, 0],
            device_id={"dp": partner}, device_id_type=MESH,
        )

    square = chips == 4
    near = chip + 1 - 2 * lax.rem(chip, 2)
    across = lax.rem(chip + 2, 4)
    corner = lax.rem(near + 2, 4)
    left, right, full = (0, size // 2), (size // 2, size // 2), (0, size)

    def shard_copy(g, kind, source, columns, to_chip, send, recv):
        at = gall.at[source, pl.ds(g * half, half), pl.ds(*columns)]
        own_part = pr.at[pl.ds(g * half, half), pl.ds(*columns)]
        return pltpu.make_async_remote_copy(
            src_ref=own_part if source is me else at, dst_ref=at,
            send_sem=send.at[g, kind], recv_sem=recv.at[g, kind],
            device_id={"dp": to_chip}, device_id_type=MESH,
        )

    def square_copies(g):
        to_near, to_across = near * 2 + core, across * 2 + core
        hops = [
            shard_copy(g, 0, me, left, to_near, gs_sem, gr_sem),
            shard_copy(g, 1, me, right, to_across, gs_sem, gr_sem),
            shard_copy(g, 2, me, right, to_near, gs_sem, gr_sem),
            shard_copy(g, 3, me, left, to_across, gs_sem, gr_sem),
            shard_copy(g, 4, to_near, left, to_across, gs_sem, gr_sem),
            shard_copy(g, 5, to_across, right, to_near, gs_sem, gr_sem),
        ]
        shares = [
            shard_copy(g, i, source, full, partner, rs_sem, rr_sem)
            for i, source in enumerate((me, to_near, to_across, corner * 2 + core))
        ]
        return hops, shares

    for side in sides:
        side.wait()
    for g in range(groups):
        run(0, CHUNKS, functools.partial(decode, g))
        slots = slice(g * half, (g + 1) * half)
        grads = transform([sums[c, slots] for c in range(tiles)], hmat[...])
        for c in range(tiles):
            cut = slice(c * TILE, (c + 1) * TILE)
            grad = grads[c] * flip[:, cut]
            master = mst[slots, cut]
            first = first_decay * fm[slots, cut] + (1.0 - first_decay) * grad
            second = second_decay * sm[slots, cut] + (1.0 - second_decay) * grad * grad
            fresh = master - learning_rate * (first / (jnp.sqrt(second) + adam_epsilon) + weight_decay * master)
            uf[slots, cut] = first
            us[slots, cut] = second
            um[slots, cut] = fresh
            pr[slots, cut] = fresh.astype(jnp.bfloat16)
        if square:
            hops, shares = square_copies(g)
            for hop in hops[:4]:
                hop.start()
            shares[0].start()
        else:
            run(1, chips, lambda c: gather_copy(g, c).start())
            own_relay(g).start()
    outs = [
        pltpu.make_async_copy(src, dst, side_sem.at[3 + i])
        for i, (src, dst) in enumerate(((um, um_hbm), (uf, uf_hbm), (us, us_hbm), (pr, gall.at[me])))
    ]
    for out in outs:
        out.start()

    for g in range(groups):
        def relay(c):
            gather_copy(g, c).wait_recv()
            relay_copy(g, c).start()

        if square:
            hops, shares = square_copies(g)
            hops[0].wait_recv()
            hops[4].start()
            hops[1].wait_recv()
            hops[5].start()
        else:
            run(1, chips, relay)
    if square:
        for g in range(groups):
            hops, shares = square_copies(g)
            hops[2].wait_recv()
            shares[1].start()
            hops[3].wait_recv()
            shares[2].start()
        for g in range(groups):
            hops, shares = square_copies(g)
            hops[4].wait_recv()
            hops[5].wait_recv()
            shares[3].start()
    for g in range(groups):
        if square:
            hops, shares = square_copies(g)
            for share in shares:
                share.wait()
            for hop in hops:
                hop.wait_send()
        else:
            own_relay(g).wait()
            run(1, chips, lambda c: relay_copy(g, c).wait())
            run(1, chips, lambda c: gather_copy(g, c).wait_send())
        run(0, CHUNKS, lambda q: run(1, n, lambda k: symbol_copy(g, q, k).wait_send()))
    run(1, n, lambda k: peak_copy(k).wait_send())
    for out in outs:
        out.wait()


def spread_kernel(layout_ref, gall_ref, um_in, uf_in, us_in, um_out, uf_out, us_out, out_ref):
    blocks = layout_ref.shape[1]
    rows = lax.broadcasted_iota(jnp.int32, (blocks, blocks), 0)
    table = (rows == layout_ref[...]).astype(jnp.float32).astype(jnp.bfloat16)
    out_ref[...] = jnp.dot(table, gall_ref[...], preferred_element_type=jnp.float32).astype(jnp.bfloat16)
    um_out[...] = um_in[...]
    uf_out[...] = uf_in[...]
    us_out[...] = us_in[...]


def local(n, gradient, dither, sign_bits, levels, layout, master, first_moment, second_moment):
    blocks, size = gradient.shape[2:]
    own = blocks // n
    tiles = size // TILE
    row_chunks = 4
    groups = slot_groups(own)
    f32, bf16 = jnp.float32, jnp.bfloat16
    hbm = pl.BlockSpec(memory_space=pl.ANY)
    vmem = pl.BlockSpec(memory_space=pltpu.VMEM)
    dma = pltpu.SemaphoreType.DMA
    layout_row = layout.reshape(1, blocks)
    shard = jax.ShapeDtypeStruct((own, size), f32)
    um, uf, us, gall = pl.pallas_call(
        functools.partial(step_kernel, n),
        out_shape=(shard, shard, shard, jax.ShapeDtypeStruct((n, own, size), bf16)),
        in_specs=[hbm, hbm, vmem, pl.BlockSpec(memory_space=pltpu.SMEM), vmem, hbm, hbm, hbm],
        out_specs=(hbm, hbm, hbm, hbm),
        scratch_shapes=[
            pltpu.VMEM((blocks, size), f32),
            pltpu.VMEM((tiles, blocks, TILE), jnp.int32),
            pltpu.VMEM((tiles, blocks, TILE), f32),
            pltpu.VMEM((blocks, blocks), f32),
            pltpu.VMEM((TILE, TILE), bf16),
            pltpu.VMEM((1, size), f32),
            pltpu.VMEM((blocks, LANES), f32),
            pltpu.VMEM((8, blocks), f32),
            pltpu.VMEM((n, 8, blocks), f32),
            pltpu.VMEM((blocks, TILE), bf16),
            pltpu.VMEM((tiles, n, own, TILE), bf16),
            pltpu.VMEM((tiles, n, own, TILE), bf16),
            pltpu.VMEM((tiles, own, TILE), f32),
            *[pltpu.VMEM((own, size), f32)] * 6,
            pltpu.VMEM((own, size), bf16),
            dma((row_chunks,)),
            dma((tiles,)),
            dma((7,)),
            dma((n,)),
            dma((n,)),
            dma((groups, CHUNKS, n)),
            dma((groups, CHUNKS, n)),
            *[dma((groups, max(6, n // 2)))] * 4,
        ],
        compiler_params=pltpu.CompilerParams(
            collective_id=0, has_side_effects=True, vmem_limit_bytes=VMEM_LIMIT
        ),
    )(
        gradient[0, 0], dither[0, 0], sign_bits.reshape(1, size), levels, layout_row,
        master[0], first_moment[0], second_moment[0],
    )
    width = size // 2
    wide = pl.BlockSpec((blocks, width), lambda i: (0, i))
    narrow = pl.BlockSpec((own, width), lambda i: (0, i))
    um, uf, us, parameters = pl.pallas_call(
        spread_kernel,
        grid=(2,),
        out_shape=(shard, shard, shard, jax.ShapeDtypeStruct((blocks, size), bf16)),
        in_specs=[pl.BlockSpec((1, blocks), lambda i: (0, 0)), wide, narrow, narrow, narrow],
        out_specs=(narrow, narrow, narrow, wide),
    )(layout_row, gall.reshape(blocks, size), um, uf, us)
    return um[None], uf[None], us[None], parameters[None]


def solution(mesh):
    slots = P("section", "dp", None)
    streams = P("section", "dp", None, None)
    return jax.shard_map(
        functools.partial(local, mesh.shape["dp"]),
        mesh=mesh,
        in_specs=(streams, streams, P(), P(), P(), slots, slots, slots),
        out_specs=(slots, slots, slots, P("section", None, None)),
        check_vma=False,
    )
```
